32 devices in a mesh: orb: 4 (over z), tile: 8 (over y, x, core).
Axes of the slice: x: 2, y: 2, z: 4, core: 2. Of those that a mesh axis runs over, the one named last changes fastest.
Arguments:
- basis_values: bfloat16 [2048, 65536], P('tile'), may hold values from -6 to 6
- coefficients: bfloat16 [65536, 128], P('tile', 'orb'), may hold values from -0.03125 to 0.03125
- occupations: float32 [128], P('orb'), may hold values from 0.5 to 2
- owners: int32 [2048, 1], P('tile'), may hold values from 0 to 7; in each aligned block of 256 rows (0 to 255, 256 to 511, ...) at most 64 rows name the same one
- offsets: int32 [2048], P('tile'), may hold values from 0 to 8191
Outputs:
- density: float32 [64, 64, 128], P('tile', 'orb')
- gradient: float32 [3, 64, 64, 128], P(None, 'tile', 'orb')
The draws below stay inside these ranges and needn't reach their ends.
Inputs may be any that keep to these rules, and one draw needn't show every extreme that they name: `owners`: at most 64 entries of one tile's list name the same owner, and some tile's list reaches 64.
All inputs are finite; a program needn't handle non-finite values.
Results may differ from the reference program's by a relative error of at most 0.0003.
Values may be sent and summed in bfloat16 or wider, within the bound.
A program may use at most 320 MiB of HBM per device.

```python
import math
import jax
import jax.numpy as jnp
import numpy as np
from jax import lax

NBT = 256
NORB = 128
ROWS_DEV = 8192
CY = 64
CZ = 128
NTILES = 8
CAP = 64
CELLS = 65536
NX = 64
NBASIS = 65536


def set_ends(values, key, least, largest):
    longest = values.shape.index(max(values.shape))
    spots = []
    for shift in (0, 1):
        where = [jax.random.randint(jax.random.fold_in(key, axis), (), 0, length) for axis, length in enumerate(values.shape)]
        where[longest] = (where[longest] + shift) % values.shape[longest]
        spots.append(tuple(where))
    return values.at[spots[0]].set(least).at[spots[1]].set(largest)


def steps_of(stream_key, dims, shards, smallest, largest):
    def one(axis_at, blocks):
        steps = jax.random.uniform(jax.random.fold_in(jax.random.fold_in(stream_key, 6), axis_at), (blocks,), jnp.float32, smallest / len(shards), largest / len(shards))
        return jnp.repeat(jnp.exp(steps), dims[axis_at] // blocks).reshape((-1,) + (1,) * (len(dims) - axis_at - 1))

    factor_of = one(*shards[0])
    for cut in shards[1:]:
        factor_of = factor_of * one(*cut)
    return factor_of


def assign_block(own_key, own, number, rows, count, top, limit, skew):
    order = jax.random.permutation(own_key, count)
    packed, usual = load_shares(count, rows * top, limit, skew, True), load_shares(count, rows * top, limit, skew, False)
    places = jnp.arange(count)

    def named(sizes, turn):
        used = int((sizes > 0).sum())
        fixed = max(1, used // 4)
        shifted = fixed + (places - fixed + turn * (used - fixed)) % max(1, count - fixed)
        return jnp.zeros((count,), jnp.int32).at[order[jnp.where(places < fixed, places, shifted)]].set(jnp.asarray(sizes, jnp.int32))

    sizes = jnp.where(number % 4 == 0, named(packed, number // 4), named(usual, number - number // 4 - 1))
    mixed = jax.random.permutation(jax.random.fold_in(own, 3), count)
    donor, receiver = mixed[0:count // 2 * 2:2], mixed[1:count // 2 * 2:2]
    slack = jnp.minimum(sizes[donor] - 1, limit - sizes[receiver]) // 2
    slack = jnp.where((donor == order[0]) | (receiver == order[0]) | (sizes[receiver] == 0), 0, jnp.maximum(slack, 0))
    shifted = jax.random.randint(jax.random.fold_in(own, 4), (count // 2,), 0, 1 << 20) % (slack + 1)
    sizes = sizes.at[donor].add(-shifted).at[receiver].add(shifted)
    members = jnp.searchsorted(jnp.cumsum(sizes), jnp.arange(rows * top), side="right").astype(jnp.int32)
    listing = members.reshape(top, rows).T
    listing = listing[jax.random.permutation(jax.random.fold_in(own, 1), rows)]
    turn = jax.random.randint(jax.random.fold_in(own, 2), (rows, 1), 0, top)
    return jnp.take_along_axis(listing, (jnp.arange(top)[None, :] + turn) % top, axis=1)


def load_shares(amount, total, bound, slope, full):
    weights = [(1 << 20) // math.isqrt(rank ** slope) + 1 for rank in range(1, amount + 1)]
    largest = bound if full else min(bound, max(-(-total // amount), total * weights[0] // sum(weights)))
    least = 1 if total - largest >= amount - 1 else 0
    given, spare = [largest] + [least] * (amount - 1), total - largest - least * (amount - 1)
    while spare > 0:
        candidates = [i for i in range(1, amount) if given[i] < largest] or [i for i in range(1, amount) if given[i] < bound]
        whole, budget = sum([weights[i] for i in candidates]), spare
        for i in candidates:
            more = min(bound - given[i], max(1, budget * weights[i] // whole), spare)
            given[i] = given[i] + more
            spare = spare - more
    return np.array(given)


def bell_draw(own_key, extent, deviation, bound, shards=(), kind=jnp.bfloat16):
    values = jax.random.normal(own_key, extent, jnp.float32) * deviation
    if len(shards) > 0:
        values = steps_of(own_key, extent, shards, -0.22, 0.18) * values
    return jnp.clip(values, min=-bound, max=bound).astype(kind)


def setup_inputs(seed: int = 0) -> dict:
    keys = jax.random.split(jax.random.key(seed), 6)
    basis_values = bell_draw(keys[0], (NTILES * NBT, CELLS), 1.0, 6.0, ((0, 8),))
    coefficients = bell_draw(keys[1], (NBASIS, NORB), (NBT * NORB) ** -0.5, 0.03125, ((0, 8), (1, 4)))
    occupations = jnp.clip(0.5 + 1.5 * jax.random.uniform(keys[2], (NORB,), jnp.float32) ** steps_of(keys[2], (NORB,), ((0, 4),), -0.2, 0.2), 0.5, 2.0)
    owners_keys = jax.random.split(jax.random.fold_in(keys[3], 1), (NTILES * NBT) // NBT)
    owners_turns = jax.random.permutation(jax.random.fold_in(keys[3], 3), (NTILES * NBT) // NBT)
    owners = jax.vmap(lambda own, number: assign_block(jax.random.fold_in(keys[3], 2), own, number, NBT, NTILES, 1, CAP, 2))(owners_keys, owners_turns).reshape((NTILES * NBT, 1))
    offsets = set_ends(jax.random.randint(keys[4], (NTILES * NBT,), 0, ROWS_DEV), jax.random.fold_in(keys[4], 1), 0, ROWS_DEV - 1).astype(jnp.int32)
    return dict(basis_values=basis_values, coefficients=coefficients, occupations=occupations, owners=owners, offsets=offsets)


def central(padded):
    along_x = 0.5 * (padded[2:, 1:-1, 1:-1] - padded[:-2, 1:-1, 1:-1])
    along_y = 0.5 * (padded[1:-1, 2:, 1:-1] - padded[1:-1, :-2, 1:-1])
    along_z = 0.5 * (padded[1:-1, 1:-1, 2:] - padded[1:-1, 1:-1, :-2])
    return jnp.stack([along_x, along_y, along_z])


def reference(basis_values, coefficients, occupations, owners, offsets):
    row_index = (owners[:, 0] * ROWS_DEV + offsets).astype(jnp.int32)
    listed = jnp.take(coefficients, row_index, axis=0).reshape(NTILES, NBT, NORB)
    values = basis_values.reshape(NTILES, NBT, CELLS)

    def one_tile(tile_pair):
        tile_rows, tile_values = tile_pair
        orbitals = jnp.dot(tile_rows.T, tile_values, preferred_element_type=jnp.float32)
        return jnp.sum(occupations[:, None] * orbitals * orbitals, axis=0)

    density = lax.map(one_tile, (listed, values)).reshape(NX, CY, CZ)
    padded = jnp.pad(density, 1)
    return density, central(padded)
```

```python
import functools

import jax
import jax.numpy as jnp
from jax import lax
from jax.experimental import pallas as pl
from jax.experimental.pallas import tpu as pltpu
from jax.sharding import PartitionSpec as P

CY = 64
CZ = 128
LANES = 128
MESH = pl.DeviceIdType.MESH
F32 = jnp.float32
BF16 = jnp.bfloat16


def iota(shape, dim):
    return lax.broadcasted_iota(jnp.int32, shape, dim)


def kernel(
    n, m, owners_ref, offsets_ref, occ_ref, coef_ref, basis_ref, dens_ref, grad_ref,
    slabs, coef, req_out, req_in, picked, rows, place, occ_in, listed, dens,
    slab_sem, coef_sem, req_send, req_recv, row_send, row_recv,
    occ_send, occ_recv, list_send, list_recv, halo_send, halo_recv,
):
    t = lax.axis_index("tile")
    o = lax.axis_index("orb")
    nbt = owners_ref.shape[1]
    held = coef_ref.shape[1]
    loc = coef_ref.shape[0]
    depth = basis_ref.shape[1] // (CY * CZ)
    width = CY // m
    inner = width * CZ
    cap = 2 * nbt // n
    per = LANES // cap
    groups = n // per
    order = [0, depth - 1] + list(range(1, depth - 1))

    coef_copy = pltpu.make_async_copy(coef_ref, coef, coef_sem)
    coef_copy.start()
    low = (o * width + CY - 1) % CY
    high = (o * width + width) % CY

    def slab_copies(x):
        out = []
        for k, (row, count, at) in enumerate(
            ((o * width, width, CZ), (low, 1, 0), (high, 1, CZ + inner))
        ):
            src = basis_ref.at[:, pl.ds(pl.multiple_of((x * CY + row) * CZ, CZ), count * CZ)]
            dst = slabs.at[x, :, pl.ds(at, count * CZ)]
            out.append(pltpu.make_async_copy(src, dst, slab_sem.at[x, k]))
        return out

    for x in order:
        for copy in slab_copies(x):
            copy.start()

    dens[0] = jnp.zeros(dens.shape[1:], F32)
    dens[depth + 1] = jnp.zeros(dens.shape[1:], F32)

    barrier = pltpu.get_barrier_semaphore()
    for d in range(1, n):
        pl.semaphore_signal(barrier, inc=1, device_id={"tile": (t + d) % n}, device_id_type=MESH)
    for d in range(1, m):
        pl.semaphore_signal(barrier, inc=1, device_id={"orb": (o + d) % m}, device_id_type=MESH)

    own = owners_ref[...]
    off = offsets_ref[...]
    named = own == iota((n, nbt), 0)
    before = (iota((nbt, nbt), 0) < iota((nbt, nbt), 1)).astype(F32).astype(BF16)
    rank = jnp.dot(named.astype(F32).astype(BF16), before, preferred_element_type=F32)
    slot = jnp.sum(jnp.where(named, rank, 0.0), axis=0, keepdims=True).astype(jnp.int32)
    slot = slot + (t % per) * cap
    spot = (slot == iota((LANES, nbt), 0)).astype(F32).astype(BF16)
    named_f = named.astype(F32)
    high_part = (named_f * (off // LANES).astype(F32)).astype(BF16)
    low_part = (named_f * (off % LANES).astype(F32)).astype(BF16)
    nt = (((1,), (1,)), ((), ()))
    req_high = lax.dot_general(high_part, spot, nt, preferred_element_type=F32)
    req_low = lax.dot_general(low_part, spot, nt, preferred_element_type=F32)
    req = (req_high * float(LANES) + req_low).astype(jnp.int32)
    for d in range(n):
        req_out[d] = jnp.broadcast_to(req[d:d + 1], (8, LANES))
    req_in[t] = req_out[t]
    row_pad = jnp.concatenate([occ_ref[...], jnp.zeros((1, LANES - loc), F32)], axis=1)
    occ_in[o] = jnp.broadcast_to(row_pad, (8, LANES))

    pl.semaphore_wait(barrier, n + m - 2)

    def req_copy(src, dst):
        return pltpu.make_async_remote_copy(
            src_ref=req_out.at[dst], dst_ref=req_in.at[src], send_sem=req_send.at[dst],
            recv_sem=req_recv.at[src], device_id={"tile": dst}, device_id_type=MESH)

    def occ_copy(src, dst):
        return pltpu.make_async_remote_copy(
            src_ref=occ_in.at[src], dst_ref=occ_in.at[src], send_sem=occ_send.at[dst],
            recv_sem=occ_recv.at[src], device_id={"orb": dst}, device_id_type=MESH)

    def row_copy(src, dst):
        return pltpu.make_async_remote_copy(
            src_ref=picked.at[dst // per],
            dst_ref=rows.at[:, pl.ds(pl.multiple_of(src * LANES, LANES), LANES)],
            send_sem=row_send.at[dst], recv_sem=row_recv.at[src],
            device_id={"tile": dst}, device_id_type=MESH)

    def list_copy(src, dst):
        return pltpu.make_async_remote_copy(
            src_ref=listed.at[src], dst_ref=listed.at[src], send_sem=list_send.at[dst],
            recv_sem=list_recv.at[src], device_id={"orb": dst}, device_id_type=MESH)

    for d in range(1, n):
        req_copy(t, (t + d) % n).start()
    for d in range(1, m):
        occ_copy(o, (o + d) % m).start()

    key = own * LANES + slot
    for d in range(n):
        here = key == iota((LANES, nbt), 0) + d * LANES
        place[d * LANES:(d + 1) * LANES, :] = here.astype(F32).astype(BF16)

    coef_copy.wait()
    for d in range(1, n):
        req_copy((t + d) % n, t).wait_recv()

    wanted = []
    for g in range(groups):
        total = req_in[g * per]
        for k in range(1, per):
            total = total + req_in[g * per + k]
        wanted.append(total)
    lane = [w % LANES for w in wanted]
    chunk_of = [w // LANES for w in wanted]
    parts = loc // 8

    def pick(h, accs):
        block = coef[:, pl.ds(pl.multiple_of(h * LANES, LANES), LANES)].astype(F32)
        out = []
        for g in range(groups):
            hit = chunk_of[g] == h
            for p in range(parts):
                got = jnp.take_along_axis(
                    block[p * 8:(p + 1) * 8], lane[g], axis=1, mode="promise_in_bounds")
                out.append(jnp.where(hit, got, accs[g * parts + p]))
        return tuple(out)

    accs = lax.fori_loop(
        0, held // LANES, pick, (jnp.zeros((8, LANES), F32),) * (groups * parts), unroll=4)
    for g in range(groups):
        picked[g] = jnp.concatenate(accs[g * parts:(g + 1) * parts], axis=0).astype(BF16)
    for d in range(1, n):
        row_copy(t, (t + d) % n).start()
    rows[:, pl.ds(pl.multiple_of(t * LANES, LANES), LANES)] = picked[t // per]
    for d in range(1, n):
        row_copy((t + d) % n, t).wait_recv()

    placed = jnp.dot(rows[...], place[...], preferred_element_type=F32)
    listed[o] = placed.astype(BF16)
    for d in range(1, m):
        list_copy(o, (o + d) % m).start()

    for d in range(1, m):
        occ_copy((o + d) % m, o).wait_recv()
    diagonal = iota((loc, LANES), 0) == iota((loc, LANES), 1)
    occ = jnp.concatenate(
        [jnp.sum(jnp.where(diagonal, occ_in[k, 0:1, :], 0.0), axis=1, keepdims=True)
         for k in range(m)], axis=0)
    occ = jnp.broadcast_to(occ, (m * loc, LANES))

    for d in range(1, m):
        list_copy((o + d) % m, o).wait_recv()
    left = listed[...].reshape(m * loc, nbt)
    count = width + 2

    def slab(x):
        for copy in slab_copies(x):
            copy.wait()
        for c in range(0, count, 2):
            orbitals = jnp.dot(
                left, slabs[x, :, c * CZ:(c + 2) * CZ], preferred_element_type=F32)
            for k in range(2):
                half = orbitals[:, k * CZ:(k + 1) * CZ]
                line = jnp.sum(half * half * occ, axis=0, keepdims=True)
                if c + k == 0:
                    line = jnp.where(o == 0, 0.0, line)
                if c + k == count - 1:
                    line = jnp.where(o == m - 1, 0.0, line)
                dens[x + 1, 7 + c + k:8 + c + k, :] = line

    def halo_copy(up):
        dst = t + 1 if up else t - 1
        return pltpu.make_async_remote_copy(
            src_ref=dens.at[depth if up else 1, pl.ds(8, width)],
            dst_ref=dens.at[0 if up else depth + 1, pl.ds(8, width)],
            send_sem=halo_send.at[int(up)], recv_sem=halo_recv.at[int(up)],
            device_id={"tile": (dst + n) % n}, device_id_type=MESH)

    slab(0)

    @pl.when(t > 0)
    def _():
        halo_copy(False).start()

    slab(depth - 1)

    @pl.when(t < n - 1)
    def _():
        halo_copy(True).start()

    def middle(x, _):
        slab(x)
        return 0

    lax.fori_loop(1, depth - 1, middle, 0)

    def gradient(x):
        rest = dens[x + 1, 8:8 + width, :]
        dens_ref[x] = rest
        grad_ref[0, x] = 0.5 * (dens[x + 2, 8:8 + width, :] - dens[x, 8:8 + width, :])
        grad_ref[1, x] = 0.5 * (dens[x + 1, 9:9 + width, :] - dens[x + 1, 7:7 + width, :])
        z = iota((width, CZ), 1)
        after = jnp.where(z == CZ - 1, 0.0, pltpu.roll(rest, CZ - 1, 1))
        prior = jnp.where(z == 0, 0.0, pltpu.roll(rest, 1, 1))
        grad_ref[2, x] = 0.5 * (after - prior)

    for x in range(1, depth - 1):
        gradient(x)

    @pl.when(t < n - 1)
    def _():
        halo_copy(False).wait_recv()

    @pl.when(t > 0)
    def _():
        halo_copy(True).wait_recv()

    gradient(0)
    gradient(depth - 1)

    for d in range(1, n):
        req_copy(t, (t + d) % n).wait_send()
        row_copy(t, (t + d) % n).wait_send()
    for d in range(1, m):
        occ_copy(o, (o + d) % m).wait_send()
        list_copy(o, (o + d) % m).wait_send()

    @pl.when(t > 0)
    def _():
        halo_copy(False).wait_send()

    @pl.when(t < n - 1)
    def _():
        halo_copy(True).wait_send()


def body(n, m, basis_values, coefficients, occupations, owners, offsets):
    nbt = owners.shape[0]
    held, loc = coefficients.shape
    depth = basis_values.shape[1] // (CY * CZ)
    width = CY // m
    groups = n // (LANES * n // (2 * nbt))
    dma = pltpu.SemaphoreType.DMA
    vmem = pl.BlockSpec(memory_space=pltpu.VMEM)
    hbm = pl.BlockSpec(memory_space=pl.ANY)
    return pl.pallas_call(
        functools.partial(kernel, n, m),
        out_shape=(
            jax.ShapeDtypeStruct((depth, width, CZ), F32),
            jax.ShapeDtypeStruct((3, depth, width, CZ), F32),
        ),
        in_specs=[vmem, vmem, vmem, hbm, hbm],
        out_specs=(vmem, vmem),
        scratch_shapes=[
            pltpu.VMEM((depth, nbt, (width + 2) * CZ), BF16),
            pltpu.VMEM((loc, held), BF16),
            pltpu.VMEM((n, 8, LANES), jnp.int32),
            pltpu.VMEM((n, 8, LANES), jnp.int32),
            pltpu.VMEM((groups, loc, LANES), BF16),
            pltpu.VMEM((loc, n * LANES), BF16),
            pltpu.VMEM((n * LANES, nbt), BF16),
            pltpu.VMEM((m, 8, LANES), F32),
            pltpu.VMEM((m, loc, nbt), BF16),
            pltpu.VMEM((depth + 2, width + 16, CZ), F32),
            dma((depth, 3)), dma(()),
            dma((n,)), dma((n,)), dma((n,)), dma((n,)),
            dma((m,)), dma((m,)), dma((m,)), dma((m,)),
            dma((2,)), dma((2,)),
        ],
        compiler_params=pltpu.CompilerParams(collective_id=0, has_side_effects=True),
    )(
        owners.reshape(1, nbt), offsets.reshape(1, nbt), occupations.reshape(1, loc),
        coefficients.T, basis_values,
    )


def solution(mesh):
    n, m = mesh.shape["tile"], mesh.shape["orb"]
    placed = (P("tile", None), P("tile", "orb"), P("orb"), P("tile", None), P("tile"))
    return jax.shard_map(
        functools.partial(body, n, m),
        mesh=mesh,
        in_specs=placed,
        out_specs=(P("tile", "orb", None), P(None, "tile", "orb", None)),
        check_vma=False,
    )
```

```python
import functools

import jax
import jax.numpy as jnp
from jax import lax
from jax.experimental import pallas as pl
from jax.experimental.pallas import tpu as pltpu
from jax.sharding import PartitionSpec as P

CY = 64
CZ = 128
LANES = 128
MESH = pl.DeviceIdType.MESH
F32 = jnp.float32
BF16 = jnp.bfloat16


def iota(shape, dim):
    return lax.broadcasted_iota(jnp.int32, shape, dim)


def kernel(
    n, m, owners_ref, offsets_ref, occ_ref, coef_ref, basis_ref, dens_ref, grad_ref,
    own_in, off_in, occ_own, slabs, coef, req_out, req_in, picked, rows, place, occ_in, listed, dens,
    small_sem, slab_sem, coef_sem, req_send, req_recv, row_send, row_recv,
    occ_send, occ_recv, list_send, list_recv, halo_send, halo_recv, ready,
):
    t = lax.axis_index("tile")
    o = lax.axis_index("orb")
    nbt = owners_ref.shape[1]
    held = coef_ref.shape[1]
    loc = coef_ref.shape[0]
    depth = basis_ref.shape[1] // (CY * CZ)
    width = CY // m
    inner = width * CZ
    cap = 2 * nbt // n
    per = LANES // cap
    groups = n // per
    order = [0, depth - 1] + list(range(1, depth - 1))

    dens[0] = jnp.zeros(dens.shape[1:], F32)
    dens[depth + 1] = jnp.zeros(dens.shape[1:], F32)

    beside = ((o > 0, -1), (o < m - 1, 1))
    count_beside = jnp.where(o > 0, 1, 0) + jnp.where(o < m - 1, 1, 0)

    def tell_beside(sem):
        for has, step in beside:
            @pl.when(has)
            def _():
                pl.semaphore_signal(
                    sem, inc=1, device_id={"orb": (o + step + m) % m}, device_id_type=MESH)

    barrier = pltpu.get_barrier_semaphore()
    for d in range(1, n):
        pl.semaphore_signal(barrier, inc=1, device_id={"tile": (t + d) % n}, device_id_type=MESH)
    tell_beside(barrier)

    small = [
        pltpu.make_async_copy(src, dst, small_sem.at[k])
        for k, (src, dst) in enumerate(
            ((owners_ref, own_in), (offsets_ref, off_in), (occ_ref, occ_own)))
    ]
    for copy in small:
        copy.start()
    coef_copy = pltpu.make_async_copy(coef_ref, coef, coef_sem)
    coef_copy.start()
    low = (o * width + CY - 1) % CY
    high = (o * width + width) % CY

    def slab_copies(x):
        out = []
        for k, (row, count, at) in enumerate(
            ((o * width, width, CZ), (low, 1, 0), (high, 1, CZ + inner))
        ):
            src = basis_ref.at[:, pl.ds(pl.multiple_of((x * CY + row) * CZ, CZ), count * CZ)]
            dst = slabs.at[x, :, pl.ds(at, count * CZ)]
            out.append(pltpu.make_async_copy(src, dst, slab_sem.at[x, k]))
        return out

    for x in order:
        for copy in slab_copies(x):
            copy.start()

    for copy in small:
        copy.wait()
    own = own_in[...]
    off = off_in[...]
    named = own == iota((n, nbt), 0)
    before = (iota((nbt, nbt), 0) < iota((nbt, nbt), 1)).astype(F32).astype(BF16)
    rank = jnp.dot(named.astype(F32).astype(BF16), before, preferred_element_type=F32)
    slot = jnp.sum(jnp.where(named, rank, 0.0), axis=0, keepdims=True).astype(jnp.int32)
    slot = slot + (t % per) * cap
    spot = (slot == iota((LANES, nbt), 0)).astype(F32).astype(BF16)
    named_f = named.astype(F32)
    high_part = (named_f * (off // LANES).astype(F32)).astype(BF16)
    low_part = (named_f * (off % LANES).astype(F32)).astype(BF16)
    nt = (((1,), (1,)), ((), ()))
    req_high = lax.dot_general(high_part, spot, nt, preferred_element_type=F32)
    req_low = lax.dot_general(low_part, spot, nt, preferred_element_type=F32)
    req = (req_high * float(LANES) + req_low).astype(jnp.int32)
    for d in range(n):
        req_out[d] = jnp.broadcast_to(req[d:d + 1], (8, LANES))
    req_in[t] = req_out[t]
    row_pad = jnp.concatenate([occ_own[...], jnp.zeros((1, LANES - loc), F32)], axis=1)
    occ_in[o] = jnp.broadcast_to(row_pad, (8, LANES))

    pl.semaphore_wait(barrier, n - 1 + count_beside)

    def req_copy(src, dst):
        return pltpu.make_async_remote_copy(
            src_ref=req_out.at[dst], dst_ref=req_in.at[src], send_sem=req_send.at[dst],
            recv_sem=req_recv.at[src], device_id={"tile": dst}, device_id_type=MESH)

    def occ_copy(src, dst):
        return pltpu.make_async_remote_copy(
            src_ref=occ_in.at[src], dst_ref=occ_in.at[src], send_sem=occ_send.at[dst],
            recv_sem=occ_recv.at[src], device_id={"orb": dst}, device_id_type=MESH)

    def row_copy(turn, src, dst):
        return pltpu.make_async_remote_copy(
            src_ref=picked.at[turn],
            dst_ref=rows.at[:, pl.ds(pl.multiple_of(src * LANES, LANES), LANES)],
            send_sem=row_send.at[dst], recv_sem=row_recv.at[src],
            device_id={"tile": dst}, device_id_type=MESH)

    def list_copy(src, dst):
        return pltpu.make_async_remote_copy(
            src_ref=listed.at[src], dst_ref=listed.at[src], send_sem=list_send.at[dst],
            recv_sem=list_recv.at[src], device_id={"orb": dst}, device_id_type=MESH)

    for d in range(1, n):
        req_copy(t, (t + d) % n).start()
    if m > 2:
        tell_beside(ready.at[0])

    key = own * LANES + slot
    for d in range(n):
        here = key == iota((LANES, nbt), 0) + d * LANES
        place[d * LANES:(d + 1) * LANES, :] = here.astype(F32).astype(BF16)

    coef_copy.wait()

    home = t // per
    turns = [home, home + 1 - 2 * (home % 2), (home + 2) % groups, groups - 1 - home]
    wide = 2 * LANES
    batch = 8
    for turn, g in enumerate(turns):
        members = [g * per + k for k in range(per)]
        total = None
        for who in members:
            if turn == 0:
                @pl.when(who != t)
                def _():
                    req_copy(who, t).wait_recv()
            else:
                req_copy(who, t).wait_recv()
            total = req_in[who] if total is None else total + req_in[who]
        chunk_of = total // wide
        lane = (total % wide)[0:1]
        chosen = (iota((wide, LANES), 0) == lane).astype(F32).astype(BF16)
        acc = [jnp.zeros((8, LANES), F32)] * (loc // 8)
        for first in range(0, held // wide, batch):
            stack = jnp.concatenate(
                [coef[:, h * wide:(h + 1) * wide] for h in range(first, first + batch)], axis=0)
            found = jnp.dot(stack, chosen, preferred_element_type=F32)
            for h in range(batch):
                hit = chunk_of == first + h
                for p in range(loc // 8):
                    at = h * loc + p * 8
                    acc[p] = jnp.where(hit, found[at:at + 8], acc[p])
        picked[turn] = jnp.concatenate(acc, axis=0).astype(BF16)
        for who in members:
            if turn == 0:
                @pl.when(who != t)
                def _():
                    row_copy(turn, t, who).start()
            else:
                row_copy(turn, t, who).start()
    rows[:, pl.ds(pl.multiple_of(t * LANES, LANES), LANES)] = picked[0]

    for k in range(m - 2):
        pl.semaphore_wait(ready.at[k], count_beside)
        if k + 1 < m - 2:
            tell_beside(ready.at[k + 1])
    for d in range(1, m):
        occ_copy(o, (o + d) % m).start()

    for d in range(1, n):
        row_copy(0, (t + d) % n, t).wait_recv()

    placed = jnp.dot(rows[...], place[...], preferred_element_type=F32)
    listed[o] = placed.astype(BF16)
    for d in range(1, m):
        list_copy(o, (o + d) % m).start()

    for d in range(1, m):
        occ_copy((o + d) % m, o).wait_recv()
    diagonal = iota((loc, LANES), 0) == iota((loc, LANES), 1)
    occ = jnp.concatenate(
        [jnp.sum(jnp.where(diagonal, occ_in[k, 0:1, :], 0.0), axis=1, keepdims=True)
         for k in range(m)], axis=0)
    occ = jnp.broadcast_to(occ, (m * loc, LANES))

    for d in range(1, m):
        list_copy((o + d) % m, o).wait_recv()
    left = listed[...].reshape(m * loc, nbt)
    count = width + 2

    def slab(x):
        for copy in slab_copies(x):
            copy.wait()
        for c in range(0, count, 2):
            orbitals = jnp.dot(
                left, slabs[x, :, c * CZ:(c + 2) * CZ], preferred_element_type=F32)
            for k in range(2):
                half = orbitals[:, k * CZ:(k + 1) * CZ]
                line = jnp.sum(half * half * occ, axis=0, keepdims=True)
                if c + k == 0:
                    line = jnp.where(o == 0, 0.0, line)
                if c + k == count - 1:
                    line = jnp.where(o == m - 1, 0.0, line)
                dens[x + 1, 7 + c + k:8 + c + k, :] = line

    def halo_copy(up):
        dst = t + 1 if up else t - 1
        return pltpu.make_async_remote_copy(
            src_ref=dens.at[depth if up else 1, pl.ds(8, width)],
            dst_ref=dens.at[0 if up else depth + 1, pl.ds(8, width)],
            send_sem=halo_send.at[int(up)], recv_sem=halo_recv.at[int(up)],
            device_id={"tile": (dst + n) % n}, device_id_type=MESH)

    slab(0)

    @pl.when(t > 0)
    def _():
        halo_copy(False).start()

    slab(depth - 1)

    @pl.when(t < n - 1)
    def _():
        halo_copy(True).start()

    def middle(x, _):
        slab(x)
        return 0

    lax.fori_loop(1, depth - 1, middle, 0)

    def gradient(x):
        rest = dens[x + 1, 8:8 + width, :]
        dens_ref[x] = rest
        grad_ref[0, x] = 0.5 * (dens[x + 2, 8:8 + width, :] - dens[x, 8:8 + width, :])
        grad_ref[1, x] = 0.5 * (dens[x + 1, 9:9 + width, :] - dens[x + 1, 7:7 + width, :])
        z = iota((width, CZ), 1)
        after = jnp.where(z == CZ - 1, 0.0, pltpu.roll(rest, CZ - 1, 1))
        prior = jnp.where(z == 0, 0.0, pltpu.roll(rest, 1, 1))
        grad_ref[2, x] = 0.5 * (after - prior)

    for x in range(1, depth - 1):
        gradient(x)

    @pl.when(t < n - 1)
    def _():
        halo_copy(False).wait_recv()

    @pl.when(t > 0)
    def _():
        halo_copy(True).wait_recv()

    gradient(0)
    gradient(depth - 1)

    for d in range(1, n):
        req_copy(t, (t + d) % n).wait_send()
        row_copy(0, t, (t + d) % n).wait_send()
    for d in range(1, m):
        occ_copy(o, (o + d) % m).wait_send()
        list_copy(o, (o + d) % m).wait_send()

    @pl.when(t > 0)
    def _():
        halo_copy(False).wait_send()

    @pl.when(t < n - 1)
    def _():
        halo_copy(True).wait_send()


def body(n, m, basis_values, coefficients, occupations, owners, offsets):
    nbt = owners.shape[0]
    held, loc = coefficients.shape
    depth = basis_values.shape[1] // (CY * CZ)
    width = CY // m
    groups = n // (LANES * n // (2 * nbt))
    dma = pltpu.SemaphoreType.DMA
    vmem = pl.BlockSpec(memory_space=pltpu.VMEM)
    hbm = pl.BlockSpec(memory_space=pl.ANY)
    return pl.pallas_call(
        functools.partial(kernel, n, m),
        out_shape=(
            pltpu.VMEM((depth, width, CZ), F32),
            pltpu.VMEM((3, depth, width, CZ), F32),
        ),
        in_specs=[hbm] * 5,
        out_specs=(vmem, vmem),
        scratch_shapes=[
            pltpu.VMEM((1, nbt), jnp.int32),
            pltpu.VMEM((1, nbt), jnp.int32),
            pltpu.VMEM((1, loc), F32),
            pltpu.VMEM((depth, nbt, (width + 2) * CZ), BF16),
            pltpu.VMEM((loc, held), BF16),
            pltpu.VMEM((n, 8, LANES), jnp.int32),
            pltpu.VMEM((n, 8, LANES), jnp.int32),
            pltpu.VMEM((groups, loc, LANES), BF16),
            pltpu.VMEM((loc, n * LANES), BF16),
            pltpu.VMEM((n * LANES, nbt), BF16),
            pltpu.VMEM((m, 8, LANES), F32),
            pltpu.VMEM((m, loc, nbt), BF16),
            pltpu.VMEM((depth + 2, width + 16, CZ), F32),
            dma((3,)), dma((depth, 3)), dma(()),
            dma((n,)), dma((n,)), dma((n,)), dma((n,)),
            dma((m,)), dma((m,)), dma((m,)), dma((m,)),
            dma((2,)), dma((2,)), pltpu.SemaphoreType.REGULAR((max(1, m - 2),)),
        ],
        compiler_params=pltpu.CompilerParams(collective_id=0, has_side_effects=True),
    )(
        owners.reshape(1, nbt), offsets.reshape(1, nbt), occupations.reshape(1, loc),
        coefficients.T, basis_values,
    )


def solution(mesh):
    n, m = mesh.shape["tile"], mesh.shape["orb"]
    placed = (P("tile", None), P("tile", "orb"), P("orb"), P("tile", None), P("tile"))
    return jax.shard_map(
        functools.partial(body, n, m),
        mesh=mesh,
        in_specs=placed,
        out_specs=(P("tile", "orb", None), P(None, "tile", "orb", None)),
        check_vma=False,
    )
```
